32 devices in a mesh: sub: 16 (over z, y, x), row: 2 (over core).
Axes of the slice: x: 2, y: 2, z: 4, core: 2. Of those that a mesh axis runs over, the one named last changes fastest.
Arguments:
- gap_field: float32 [4, 16, 8192], P(None, 'sub', 'row'), may hold values from -6 to 6
- flex_diag: float32 [16, 8192], P('sub', 'row'), may hold values from 0.5 to 4
- schur_diag: float32 [16, 8192], P('sub', 'row'), may hold values from 0.5 to 4
- schur_factor: bfloat16 [16, 128, 64, 512], P('sub', 'row'), may hold values from -0.25 to 0.25
- block_offsets: int32 [8], replicated, may hold values from 0 to 127, as said below
- coarse_basis: float32 [16, 12, 8192], P('sub', None, 'row'), may hold values from -0.5 to 0.5
- coarse_factor: float32 [75, 75], replicated, may hold values from -0.75 to 0.75
Outputs:
- multipliers: float32 [4, 16, 8192], P(None, 'sub', 'row')
- residual: float32 [4, 16, 8192], P(None, 'sub', 'row')
The draws below stay inside these ranges and needn't reach their ends.
Inputs may be any that keep to these rules, and one draw needn't show every extreme that they name: `block_offsets`: 8 distinct block offsets shared by all subdomains; 0 and 127 are always among them.
All inputs are finite; a program needn't handle non-finite values.
Results may differ from the reference program's by a relative error of at most 0.0021.
Values may be sent and summed in bfloat16 or wider, within the bound.
A program may use at most 64 MiB of HBM per device.

```python
import math
import jax
import jax.numpy as jnp
from jax import lax

NI = 8192
BLOCK = 64
K = 8
CD = 3
ITERS = 2
LOADS = 4
SUBS = 16
NB = 128
FQ = 1024
CS = 12
NP = 75
N_ROW = 2


def draw_block_offsets(key, part):
    inner_offsets = jax.random.permutation(key, NB - 2)[:K - 2] + 1
    return jnp.concatenate([jnp.array([0, NB - 1], jnp.int32), inner_offsets.astype(jnp.int32)])


def levels(key, dims, shards, least, high):
    level, own = 1.0, jax.random.fold_in(key, 6)
    for position, blocks in shards:
        heights = jnp.exp(jax.random.uniform(jax.random.fold_in(own, position), (blocks,), jnp.float32, least / len(shards), high / len(shards)))
        level = level * jnp.repeat(heights, dims[position] // blocks).reshape([-1 if axis == position else 1 for axis in range(len(dims))])
    return level


def scatter_about(own_key, dims, scale, limit, shards=(), dtype=jnp.bfloat16):
    drawn = jax.random.normal(own_key, dims, jnp.float32) * scale
    if len(shards) > 0:
        drawn = levels(own_key, dims, shards, -0.22, 0.18) * drawn
    return jnp.clip(drawn, min=-limit, max=limit).astype(dtype)


def setup_inputs(seed: int = 0) -> dict:
    arg_keys = jax.random.split(jax.random.key(seed), 8)
    return {
        "gap_field": scatter_about(arg_keys[0], (LOADS, SUBS, NI), 1.0, 6.0, ((1, 16), (2, 2)), jnp.float32),
        "flex_diag": jnp.clip(jnp.exp(math.log(4.0) - 2.0794415 * jax.random.uniform(arg_keys[1], (SUBS, NI), jnp.float32) ** levels(arg_keys[1], (SUBS, NI), ((0, 16), (1, 2)), -0.2, 0.2)), 0.5, 4.0),
        "schur_diag": jnp.clip(jnp.exp(math.log(4.0) - 2.0794415 * jax.random.uniform(arg_keys[2], (SUBS, NI), jnp.float32) ** levels(arg_keys[2], (SUBS, NI), ((0, 16), (1, 2)), -0.2, 0.2)), 0.5, 4.0),
        "schur_factor": scatter_about(arg_keys[3], (SUBS, NB, BLOCK, K * BLOCK), (K * BLOCK) ** -0.5, 0.25, ((0, 16), (1, 2))),
        "block_offsets": draw_block_offsets(jax.random.fold_in(arg_keys[7], 71), 0),
        "coarse_basis": scatter_about(arg_keys[5], (SUBS, CS, NI), (NI // 64) ** -0.5, 0.5, ((0, 16), (2, 2)), jnp.float32),
        "coarse_factor": scatter_about(arg_keys[6], (NP, NP), NP ** -0.5, 0.75, (), jnp.float32),
    }


highest = lax.Precision.HIGHEST


def shift_subs(values, offset):
    padding = jnp.zeros_like(values[:, :abs(offset)])
    if offset > 0:
        return jnp.concatenate([padding, values[:, :-offset]], axis=1)
    return jnp.concatenate([values[:, -offset:], padding], axis=1)


def open_faces():
    sub_ids = jnp.arange(SUBS)
    column = sub_ids % 4
    grid_row = sub_ids // 4
    return jnp.stack([column > 0, column < 3, grid_row > 0, grid_row < SUBS // 4 - 1], axis=1).astype(jnp.float32)


def jump_field(field):
    load_count = field.shape[0]
    parts = field.reshape(load_count, SUBS, N_ROW, 4, FQ)
    across = jnp.stack([shift_subs(parts[:, :, :, 1], 1), shift_subs(parts[:, :, :, 0], -1), shift_subs(parts[:, :, :, 3], 4), shift_subs(parts[:, :, :, 2], -4)], axis=3)
    result = open_faces()[None, :, None, :, None] * (parts - across)
    return result.reshape(load_count, SUBS, NI)


def schur_apply(field, schur_diag, schur_factor, block_offsets):
    block_cols = ((jnp.arange(NB)[:, None] + block_offsets[None, :]) % NB).astype(jnp.int32)

    def one_subdomain(pair):
        factor, local_field = pair
        rounded = lax.optimization_barrier(local_field.astype(jnp.bfloat16)).astype(jnp.float32)
        gathered = rounded.reshape(LOADS, NB, BLOCK)[:, block_cols].reshape(LOADS, NB, K * BLOCK)
        wide_factor = factor.astype(jnp.float32)
        block_prods = jnp.einsum('bik,lbk->lbi', wide_factor, gathered, precision=highest)
        block_prods = lax.optimization_barrier(block_prods.astype(jnp.bfloat16)).astype(jnp.float32)
        spread = jnp.einsum('bik,lbi->lbk', wide_factor, block_prods, precision=highest).reshape(LOADS, NB, K, BLOCK)
        summed = jnp.zeros((LOADS, NB, BLOCK), jnp.float32).at[:, block_cols].add(spread)
        return summed.reshape(LOADS, NI)

    mapped = lax.map(one_subdomain, (schur_factor, jnp.transpose(field, (1, 0, 2))))
    return schur_diag[None] * field + jnp.transpose(mapped, (1, 0, 2))


def slot_dofs():
    sub_ids = jnp.arange(SUBS)
    column = sub_ids % 4
    grid_row = sub_ids // 4
    nodes = jnp.stack([grid_row * 5 + column, grid_row * 5 + column + 1, (grid_row + 1) * 5 + column, (grid_row + 1) * 5 + column + 1], axis=1)
    return (nodes[:, :, None] * CD + jnp.arange(CD)[None, None, :]).reshape(SUBS, 4 * CD).astype(jnp.int32)


def coarse_apply(direction, coarse_basis, coarse_factor):
    dofs = slot_dofs()
    slot_values = jnp.einsum('sqn,lsn->lsq', coarse_basis, direction, precision=highest)
    coarse_rhs = jnp.zeros((LOADS, NP), jnp.float32).at[:, dofs.reshape(-1)].add(slot_values.reshape(LOADS, -1))
    coarse_half = jnp.dot(coarse_rhs, coarse_factor, precision=highest, preferred_element_type=jnp.float32)
    coarse_sol = jnp.dot(coarse_half, coarse_factor.T, precision=highest, preferred_element_type=jnp.float32)
    back = jnp.einsum('sqn,lsq->lsn', coarse_basis, coarse_sol[:, dofs], precision=highest)
    return back, jnp.sum(coarse_half * coarse_half, axis=1)


def reference(gap_field, flex_diag, schur_diag, schur_factor, block_offsets, coarse_basis, coarse_factor):
    def precondition(field):
        return jump_field(schur_apply(field, schur_diag, schur_factor, block_offsets))

    residual = jump_field(gap_field)
    smoothed = precondition(residual)
    res_dot = jnp.sum(residual * smoothed, axis=(1, 2))
    direction = smoothed
    multipliers = jnp.zeros_like(residual)
    for iteration in range(ITERS):
        back, coarse_energy = coarse_apply(direction, coarse_basis, coarse_factor)
        image = jump_field(flex_diag[None] * direction + back)
        curvature = 2.0 * (jnp.sum(flex_diag[None] * direction * direction, axis=(1, 2)) + coarse_energy)
        step_size = (res_dot / curvature)[:, None, None]
        multipliers = multipliers + step_size * direction
        residual = residual - step_size * image
        if iteration + 1 < ITERS:
            smoothed = precondition(residual)
            res_next = jnp.sum(residual * smoothed, axis=(1, 2))
            direction = smoothed + (res_next / res_dot)[:, None, None] * direction
            res_dot = res_next
    return multipliers, residual
```

```python
import functools
import jax
import jax.numpy as jnp
from jax import lax
from jax.experimental import pallas as pl
from jax.experimental.pallas import tpu as pltpu
from jax.sharding import PartitionSpec as P

CD = 3
COLS = 4
ITERS = 2
LANES = 128
SLOT = 16
MESH = pl.DeviceIdType.MESH
OPPOSITE = (1, 0, 3, 2)
STEPS = (-1, 1, -COLS, COLS)


def kernel(
    subs, rows, block,
    gap, fb, sd, fac_hbm, off, cf,
    mult_out, res_out,
    gapf, ac_gap, fbf, fba, fac, xd, gb, z2, un, rs, zz, pp, mm, fsum,
    part, sib, ss, ac, msg, ar, tf,
    fac_sem, own_sem, gs_s, gs_r, gf_s, gf_r, fs_s, fs_r, ff_s, ff_r,
    ps_s, ps_r, hs_s, hs_r, as_s, as_r,
):
    loads, half = gap.shape[0], gap.shape[1]
    face = half // 4
    slots = fb.shape[0] - 1
    wide = 2 * loads
    local_rows = gb.shape[0]
    all_rows = local_rows * rows
    blocks = all_rows // loads
    local_blocks = local_rows // loads
    pairs = z2.shape[0]
    whole = half * rows
    coarse = cf.shape[0]
    padded = tf.shape[1]
    me = lax.axis_index("sub")
    row = lax.axis_index("row")
    column = me % COLS
    grid_row = me // COLS
    opened = (column > 0, column < COLS - 1, grid_row > 0, grid_row < subs // COLS - 1)

    load_factor = pltpu.make_async_copy(fac_hbm, fac, fac_sem)
    load_factor.start()
    own_gap = pltpu.make_async_copy(gap, gapf.at[:, row], own_sem.at[0])
    own_fb = pltpu.make_async_copy(fb, fbf.at[:, row], own_sem.at[1])
    own_gap.start()
    own_fb.start()

    barrier = pltpu.get_barrier_semaphore()

    def greet(d, carry):
        pl.semaphore_signal(
            barrier, inc=1, device_id={"sub": (me + d) % subs, "row": row}, device_id_type=MESH
        )
        return carry

    lax.fori_loop(1, subs, greet, 0)
    expected = subs - 1 + rows - 1
    for d in range(1, rows):
        other = (row + d) % rows
        pl.semaphore_signal(barrier, inc=1, device_id={"sub": me, "row": other}, device_id_type=MESH)
        for f in range(4):

            @pl.when(opened[f])
            def _():
                pl.semaphore_signal(
                    barrier, inc=1, device_id={"sub": me + STEPS[f], "row": other}, device_id_type=MESH
                )

            expected = expected + jnp.where(opened[f], 1, 0)
    pl.semaphore_wait(barrier, expected)

    def sibling(src, dst, d, sends, receives):
        return pltpu.make_async_remote_copy(
            src_ref=src, dst_ref=dst, send_sem=sends, recv_sem=receives,
            device_id={"sub": me, "row": (row + d) % rows}, device_id_type=MESH,
        )

    def across(src, dst, f, d, sends, receives):
        return pltpu.make_async_remote_copy(
            src_ref=src, dst_ref=dst, send_sem=sends, recv_sem=receives,
            device_id={"sub": me + STEPS[f], "row": (row + d) % rows}, device_id_type=MESH,
        )

    def span(f):
        return pl.ds(f * face, face)

    def exchange_start(src, full, far, sib_s, sib_r, far_s, far_r):
        for d in range(1, rows):
            sibling(src, full.at[:, row], d, sib_s.at[d], sib_r.at[d]).start()
        for f in range(4):

            @pl.when(opened[f])
            def _():
                for d in range(rows):
                    across(
                        src.at[:, span(f)], far.at[:, row, span(OPPOSITE[f])], f, d,
                        far_s.at[f, d], far_r.at[OPPOSITE[f], d],
                    ).start()

    def exchange_wait(src, full, far, sib_s, sib_r, far_s, far_r):
        for d in range(1, rows):
            sibling(src, full.at[:, (row - d + rows) % rows], d, sib_s.at[d], sib_r.at[d]).wait()
        for f in range(4):

            @pl.when(opened[f])
            def _():
                for d in range(rows):
                    across(
                        src.at[:, span(f)], far.at[:, (row - d + rows) % rows, span(f)], f, d,
                        far_s.at[f, d], far_r.at[f, d],
                    ).wait()

    first = (gap, gapf, ac_gap, gs_s, gs_r, gf_s, gf_r)
    second = (fb, fbf, fba, fs_s, fs_r, ff_s, ff_r)
    exchange_start(*first)
    exchange_start(*second)

    tf[...] = jnp.zeros_like(tf)
    for n, step in enumerate((0,) + STEPS):
        base_col = (me + step + subs) % COLS if n in (1, 2) else column
        base_row = grid_row + (0 if n < 3 else STEPS[n - 1] // COLS)
        base_row = jnp.clip(base_row, 0, subs // COLS - 1)
        for j in range(4):
            node = (base_row + j // 2) * (COLS + 1) + base_col + j % 2
            for e in range(CD):
                slot = n * SLOT + j * CD + e
                tf[slot:slot + 1, 0:coarse] = cf[pl.ds(node * CD + e, 1), :]
    blank = jnp.zeros((all_rows - local_rows, LANES), jnp.float32)
    for pair in range(pairs):
        z2[pair, local_rows:all_rows, :] = blank
        z2[pair, all_rows + local_rows:2 * all_rows, :] = blank

    low = lax.broadcasted_iota(jnp.int32, (1, LANES), 1) < block
    faces = [jnp.full((face, LANES), jnp.where(opened[f], 1, 0), jnp.int32) > 0 for f in range(4)]
    group = 256 // block
    grp_rows = group * loads

    def jump(field, far, out):
        for l in range(loads):
            for r in range(rows):
                for f in range(4):
                    part_f = field[l, r, f * face:(f + 1) * face, :] - far[l, r, f * face:(f + 1) * face, :]
                    out[l, r, f * face:(f + 1) * face, :] = jnp.where(faces[f], part_f, 0.0)

    def schur(x, out):
        for l in range(loads):
            w = x[l].reshape(whole, LANES).astype(jnp.bfloat16).astype(jnp.float32)
            turned = pltpu.roll(w, block, 1)
            even = jnp.where(low, w, turned)
            odd = jnp.where(low, turned, w)
            for copy in range(2):
                xd[pl.ds(copy * all_rows + l, whole, stride=wide), :] = even
                xd[pl.ds(copy * all_rows + loads + l, whole, stride=wide), :] = odd
        for pair in range(pairs):
            at = [(off[2 * pair + e] + row * local_blocks) * loads for e in range(2)]
            left = xd[pl.ds(at[0], local_rows), :]
            right = xd[pl.ds(at[1], local_rows), :]
            gb[:, pair * LANES:(pair + 1) * LANES] = jnp.where(low, left, right).astype(jnp.bfloat16)
        own = (
            lax.broadcasted_iota(jnp.int32, (grp_rows, group * block), 0) // loads
            == lax.broadcasted_iota(jnp.int32, (grp_rows, group * block), 1) // block
        )

        def one(g, carry):
            at = pl.multiple_of(g * grp_rows, grp_rows)
            weights = fac[pl.ds(pl.multiple_of(g * group * block, group * block), group * block), :]
            t = lax.dot_general(
                gb[pl.ds(at, grp_rows), :], weights, (((1,), (1,)), ((), ())),
                preferred_element_type=jnp.float32,
            )
            t = jnp.where(own, t, 0.0).astype(jnp.bfloat16)
            s = jnp.dot(t, weights, preferred_element_type=jnp.float32)
            for pair in range(pairs):
                piece = s[:, pair * LANES:(pair + 1) * LANES]
                z2[pair, pl.ds(at, grp_rows), :] = piece
                z2[pair, pl.ds(all_rows + at, grp_rows), :] = piece
            return carry

        lax.fori_loop(0, local_blocks // group, one, 0, unroll=4)
        begin = [
            lax.rem(2 * blocks - off[k] - row * local_blocks, blocks) * loads for k in range(2 * pairs)
        ]
        tall = 64
        for c in range(all_rows // tall):
            sums = [0.0, 0.0]
            for pair in range(pairs):
                for e in range(2):
                    sums[e] = sums[e] + z2[pair, pl.ds(begin[2 * pair + e] + c * tall, tall), :]
            both = jnp.where(low, sums[0], sums[1])
            un[c * tall:(c + 1) * tall, :] = both + pltpu.roll(both, block, 1)
        for l in range(loads):
            even = un[pl.ds(l, whole, stride=wide), :]
            odd = un[pl.ds(loads + l, whole, stride=wide), :]
            out[l] = jnp.where(low, even, odd).reshape(rows, half, LANES)
        for l in range(loads):
            out[l, row] = out[l, row] + sd[...] * x[l, row]

    def precondition(x, phase, out):
        mine = part.at[phase]
        schur(x, mine)
        copies = [
            sibling(mine, sib.at[phase, d - 1], d, ps_s.at[phase, d], ps_r.at[phase, d])
            for d in range(1, rows)
        ]
        for copy in copies:
            copy.start()
        for copy in copies:
            copy.wait()
        total = ss.at[phase]
        for l in range(loads):
            value = mine[l]
            for d in range(rows - 1):
                value = value + sib[phase, d, l]
            total[l] = value

        def halo(f, to):
            return across(
                total.at[:, :, span(f)], ac.at[phase, :, :, span(to)], f, 0,
                hs_s.at[phase, f], hs_r.at[phase, to],
            )

        for f in range(4):

            @pl.when(opened[f])
            def _():
                halo(f, OPPOSITE[f]).start()

        for f in range(4):

            @pl.when(opened[f])
            def _():
                halo(f, f).wait()

        jump(total, ac.at[phase], out)

    lane = lax.broadcasted_iota(jnp.int32, (loads, padded), 1)

    def total_of(values):
        flat = jnp.concatenate(
            [jnp.sum(values[l].reshape(whole, LANES), axis=0, keepdims=True) for l in range(loads)], axis=0
        )
        return jnp.sum(flat, axis=1, keepdims=True)

    def assemble(phase, direction):
        z = zz[...]
        out = jnp.zeros((loads, padded), jnp.float32)
        for q in range(slots):
            out = out + total_of(z * fbf[1 + q][None]) * tf[q:q + 1, :]
        flexed = z * fbf[0][None]
        energies = [total_of(rs[...] * z), total_of(flexed * z)]
        if direction is not None:
            energies.append(total_of(flexed * direction[...]))
        for e, value in enumerate(energies):
            out = out + jnp.where(lane == coarse + e, value, 0.0)
        msg[phase] = out
        ar[phase, me] = out

        def send(d, slot):
            return pltpu.make_async_remote_copy(
                src_ref=msg.at[phase], dst_ref=ar.at[phase, slot],
                send_sem=as_s.at[phase, d], recv_sem=as_r.at[phase, d],
                device_id={"sub": (me + d) % subs, "row": row}, device_id_type=MESH,
            )

        def start(d, carry):
            send(d, me).start()
            return carry

        def wait(d, carry):
            send(d, (me - d + subs) % subs).wait()
            return carry

        lax.fori_loop(1, subs, start, 0)
        lax.fori_loop(1, subs, wait, 0)
        total = jnp.sum(ar[phase], axis=0)
        picked = [
            jnp.sum(jnp.where(lane == coarse + e, total, 0.0), axis=1, keepdims=True)
            for e in range(len(energies))
        ]
        return jnp.where(lane < coarse, total, 0.0), picked

    def spread_of(coarse_half, l):
        return jnp.sum(tf[...] * coarse_half[l:l + 1, :], axis=1, keepdims=True)

    def update(coarse_half, step, run_rows, direction, apply):
        for l in range(loads):
            back = spread_of(coarse_half, l)
            mine = [jnp.broadcast_to(back[q:q + 1, :], (face, LANES)) for q in range(slots)]
            scale = jnp.broadcast_to(step[l:l + 1, :], (face, LANES))
            for f in range(4):
                at = slice(f * face, (f + 1) * face)
                base = (1 + f) * SLOT
                theirs = [
                    jnp.broadcast_to(back[base + q:base + q + 1, :], (face, LANES)) for q in range(slots)
                ]
                for r in run_rows:
                    p = direction(l, r, at)
                    image = fsum[r, at, :] * p
                    for q in range(slots):
                        image = image + (mine[q] * fbf[1 + q, r, at, :] - theirs[q] * fba[1 + q, r, at, :])
                    apply(l, r, at, scale, p, jnp.where(faces[f], image, 0.0))

    own_gap.wait()
    exchange_wait(*first)
    jump(gapf, ac_gap, rs)
    load_factor.wait()
    precondition(rs, 0, zz)
    own_fb.wait()
    exchange_wait(*second)
    fsum[...] = fbf[0] + fba[0]
    coarse_half, (res_dot, energy) = assemble(0, None)

    def curvature(energy, coarse_half):
        return 2.0 * (energy + jnp.sum(coarse_half * coarse_half, axis=1, keepdims=True))

    step = res_dot / curvature(energy, coarse_half)
    pp[...] = zz[...]

    def apply_first(l, r, at, scale, p, image):
        mm[l, r, at, :] = scale * p
        rs[l, r, at, :] = rs[l, r, at, :] - scale * image

    update(coarse_half, step, range(rows), lambda l, r, at: pp[l, r, at, :], apply_first)
    precondition(rs, 1, zz)
    new_half, (res_new, energy_new, mixed) = assemble(1, pp)
    ratio = res_new / res_dot
    energy = energy_new + 2.0 * ratio * mixed + ratio * ratio * energy
    coarse_half = new_half + ratio * coarse_half
    step = res_new / curvature(energy, coarse_half)

    def last_direction(l, r, at):
        return zz[l, r, at, :] + ratio[l:l + 1, :] * pp[l, r, at, :]

    def apply_last(l, r, at, scale, p, image):
        mult_out[l, at, :] = mm[l, r, at, :] + scale * p
        res_out[l, at, :] = rs[l, r, at, :] - scale * image

    update(coarse_half, step, (row,), last_direction, apply_last)


def shards(subs, rows, gap_field, flex_diag, schur_diag, schur_factor, block_offsets, coarse_basis, coarse_factor):
    loads, _, unknowns = gap_field.shape
    _, local_blocks, block, width = schur_factor.shape
    slots = coarse_basis.shape[1]
    coarse = coarse_factor.shape[0]
    half = unknowns // LANES
    padded = -(-(coarse + 3) // LANES) * LANES
    gap = gap_field.reshape(loads, half, LANES)
    fb = jnp.concatenate([flex_diag[:, None], coarse_basis], axis=1).reshape(slots + 1, half, LANES)
    sd = schur_diag.reshape(half, LANES)
    factor = schur_factor.reshape(local_blocks * block, width)
    field = (loads, rows, half, LANES)
    basis = (slots + 1, rows, half, LANES)
    all_rows = local_blocks * rows * loads
    f32 = jnp.float32
    vm = pltpu.VMEM
    dma = pltpu.SemaphoreType.DMA
    in_vmem = pl.BlockSpec(memory_space=pltpu.VMEM)
    scratch = [
        vm(field, f32), vm(field, f32), vm(basis, f32), vm(basis, f32),
        vm(factor.shape, jnp.bfloat16),
        vm((2 * all_rows, LANES), f32),
        vm((local_blocks * loads, width), jnp.bfloat16),
        vm((width // LANES, 2 * all_rows, LANES), f32),
        vm((all_rows, LANES), f32),
        vm(field, f32), vm(field, f32), vm(field, f32), vm(field, f32),
        vm(field[1:], f32),
        vm((2,) + field, f32), vm((2, rows - 1) + field, f32), vm((2,) + field, f32), vm((2,) + field, f32),
        vm((2, loads, padded), f32), vm((2, subs, loads, padded), f32),
        vm((5 * SLOT, padded), f32),
        dma, dma((2,)),
        dma((rows,)), dma((rows,)), dma((4, rows)), dma((4, rows)),
        dma((rows,)), dma((rows,)), dma((4, rows)), dma((4, rows)),
        dma((2, rows)), dma((2, rows)), dma((2, 4)), dma((2, 4)),
        dma((2, subs)), dma((2, subs)),
    ]
    out = jax.ShapeDtypeStruct((loads, half, LANES), f32)
    mult, res = pl.pallas_call(
        functools.partial(kernel, subs, rows, block),
        out_shape=(out, out),
        in_specs=[
            in_vmem, in_vmem, in_vmem,
            pl.BlockSpec(memory_space=pl.ANY),
            pl.BlockSpec(memory_space=pltpu.SMEM),
            in_vmem,
        ],
        out_specs=(in_vmem, in_vmem),
        scratch_shapes=scratch,
        compiler_params=pltpu.CompilerParams(
            collective_id=0, has_side_effects=True, vmem_limit_bytes=48 * 1024 * 1024
        ),
    )(gap, fb, sd, factor, block_offsets, coarse_factor)
    return mult.reshape(gap_field.shape), res.reshape(gap_field.shape)


def solution(mesh):
    placed = (
        P(None, "sub", "row"),
        P("sub", "row"),
        P("sub", "row"),
        P("sub", "row", None, None),
        P(),
        P("sub", None, "row"),
        P(),
    )
    return jax.shard_map(
        functools.partial(shards, mesh.shape["sub"], mesh.shape["row"]),
        mesh=mesh,
        in_specs=placed,
        out_specs=(P(None, "sub", "row"), P(None, "sub", "row")),
        check_vma=False,
    )
```

```python
import functools
import jax
import jax.numpy as jnp
from jax import lax
from jax.experimental import pallas as pl
from jax.experimental.pallas import tpu as pltpu
from jax.sharding import PartitionSpec as P

CD = 3
COLS = 4
ITERS = 2
LANES = 128
SLOT = 16
MESH = pl.DeviceIdType.MESH
OPPOSITE = (1, 0, 3, 2)
STEPS = (-1, 1, -COLS, COLS)


def kernel(
    subs, rows, block,
    gap, flex_hbm, basis_hbm, sd_hbm, fac_hbm, off_hbm, cf_hbm,
    mult_out, res_out,
    sd, off, cf, gapf, ac_gap, fbf, fba, fac, xd, gb, z2, un, rs, zz, pp, mm, fsum,
    part, sib, ss, ac, msg, ar, tf,
    fac_sem, own_sem, gs_s, gs_r, gf_s, gf_r, fs_s, fs_r, ff_s, ff_r,
    ps_s, ps_r, hs_s, hs_r, as_s, as_r,
):
    loads, half = gap.shape[0], gap.shape[1]
    face = half // 4
    slots = basis_hbm.shape[0]
    wide = 2 * loads
    local_rows = gb.shape[0]
    all_rows = local_rows * rows
    blocks = all_rows // loads
    local_blocks = local_rows // loads
    pairs = z2.shape[0]
    whole = half * rows
    coarse = cf.shape[0]
    padded = tf.shape[1]
    me = lax.axis_index("sub")
    row = lax.axis_index("row")
    column = me % COLS
    grid_row = me // COLS
    opened = (column > 0, column < COLS - 1, grid_row > 0, grid_row < subs // COLS - 1)

    load_factor = pltpu.make_async_copy(fac_hbm, fac, fac_sem)
    own_gap = pltpu.make_async_copy(gap, gapf.at[:, row], own_sem.at[0])
    own_flex = pltpu.make_async_copy(flex_hbm, fbf.at[0, row], own_sem.at[1])
    own_basis = pltpu.make_async_copy(basis_hbm, fbf.at[1:, row], own_sem.at[2])
    load_sd = pltpu.make_async_copy(sd_hbm, sd, own_sem.at[3])
    load_off = pltpu.make_async_copy(off_hbm, off, own_sem.at[4])
    load_cf = pltpu.make_async_copy(cf_hbm, cf, own_sem.at[5])
    for copy in (own_gap, own_flex, own_basis, load_off, load_cf, load_sd, load_factor):
        copy.start()

    barrier = pltpu.get_barrier_semaphore()

    def greet(d, carry):
        pl.semaphore_signal(
            barrier, inc=1, device_id={"sub": (me + d) % subs, "row": row}, device_id_type=MESH
        )
        return carry

    lax.fori_loop(1, subs, greet, 0)
    expected = subs - 1 + rows - 1
    for d in range(1, rows):
        other = (row + d) % rows
        pl.semaphore_signal(barrier, inc=1, device_id={"sub": me, "row": other}, device_id_type=MESH)
        for f in range(4):

            @pl.when(opened[f])
            def _():
                pl.semaphore_signal(
                    barrier, inc=1, device_id={"sub": me + STEPS[f], "row": other}, device_id_type=MESH
                )

            expected = expected + jnp.where(opened[f], 1, 0)
    pl.semaphore_wait(barrier, expected)

    def sibling(src, dst, d, sends, receives):
        return pltpu.make_async_remote_copy(
            src_ref=src, dst_ref=dst, send_sem=sends, recv_sem=receives,
            device_id={"sub": me, "row": (row + d) % rows}, device_id_type=MESH,
        )

    def across(src, dst, f, d, sends, receives):
        return pltpu.make_async_remote_copy(
            src_ref=src, dst_ref=dst, send_sem=sends, recv_sem=receives,
            device_id={"sub": me + STEPS[f], "row": (row + d) % rows}, device_id_type=MESH,
        )

    def span(f):
        return pl.ds(f * face, face)

    def exchange_start(src, full, far, sib_s, sib_r, far_s, far_r):
        for d in range(1, rows):
            sibling(src, full.at[:, row], d, sib_s.at[d], sib_r.at[d]).start()
        for f in range(4):

            @pl.when(opened[f])
            def _():
                for d in range(rows):
                    across(
                        src.at[:, span(f)], far.at[:, row, span(OPPOSITE[f])], f, d,
                        far_s.at[f, d], far_r.at[OPPOSITE[f], d],
                    ).start()

    def exchange_wait(src, full, far, sib_s, sib_r, far_s, far_r):
        for d in range(1, rows):
            sibling(src, full.at[:, (row - d + rows) % rows], d, sib_s.at[d], sib_r.at[d]).wait()
        for f in range(4):

            @pl.when(opened[f])
            def _():
                for d in range(rows):
                    across(
                        src.at[:, span(f)], far.at[:, (row - d + rows) % rows, span(f)], f, d,
                        far_s.at[f, d], far_r.at[f, d],
                    ).wait()

    first = (gap, gapf, ac_gap, gs_s, gs_r, gf_s, gf_r)
    second = (fbf.at[:, row], fbf, fba, fs_s, fs_r, ff_s, ff_r)
    exchange_start(*first)
    own_flex.wait()
    own_basis.wait()
    exchange_start(*second)
    load_cf.wait()

    tf[...] = jnp.zeros_like(tf)
    for n, step in enumerate((0,) + STEPS):
        base_col = (me + step + subs) % COLS if n in (1, 2) else column
        base_row = grid_row + (0 if n < 3 else STEPS[n - 1] // COLS)
        base_row = jnp.clip(base_row, 0, subs // COLS - 1)
        for j in range(4):
            node = (base_row + j // 2) * (COLS + 1) + base_col + j % 2
            for e in range(CD):
                slot = n * SLOT + j * CD + e
                tf[slot:slot + 1, 0:coarse] = cf[pl.ds(node * CD + e, 1), :]
    blank = jnp.zeros((all_rows - local_rows, LANES), jnp.float32)
    for pair in range(pairs):
        z2[pair, local_rows:all_rows, :] = blank
        z2[pair, all_rows + local_rows:2 * all_rows, :] = blank

    low = lax.broadcasted_iota(jnp.int32, (1, LANES), 1) < block
    faces = [jnp.full((face, LANES), jnp.where(opened[f], 1, 0), jnp.int32) > 0 for f in range(4)]
    group = 256 // block
    grp_rows = group * loads

    def jump(field, far, out):
        for l in range(loads):
            for r in range(rows):
                for f in range(4):
                    part_f = field[l, r, f * face:(f + 1) * face, :] - far[l, r, f * face:(f + 1) * face, :]
                    out[l, r, f * face:(f + 1) * face, :] = jnp.where(faces[f], part_f, 0.0)

    def schur(x, out):
        for l in range(loads):
            w = x[l].reshape(whole, LANES).astype(jnp.bfloat16).astype(jnp.float32)
            turned = pltpu.roll(w, block, 1)
            even = jnp.where(low, w, turned)
            odd = jnp.where(low, turned, w)
            for copy in range(2):
                xd[pl.ds(copy * all_rows + l, whole, stride=wide), :] = even
                xd[pl.ds(copy * all_rows + loads + l, whole, stride=wide), :] = odd
        for pair in range(pairs):
            at = [(off[2 * pair + e] + row * local_blocks) * loads for e in range(2)]
            left = xd[pl.ds(at[0], local_rows), :]
            right = xd[pl.ds(at[1], local_rows), :]
            gb[:, pair * LANES:(pair + 1) * LANES] = jnp.where(low, left, right).astype(jnp.bfloat16)
        own = (
            lax.broadcasted_iota(jnp.int32, (grp_rows, group * block), 0) // loads
            == lax.broadcasted_iota(jnp.int32, (grp_rows, group * block), 1) // block
        )

        def one(g, carry):
            at = pl.multiple_of(g * grp_rows, grp_rows)
            weights = fac[pl.ds(pl.multiple_of(g * group * block, group * block), group * block), :]
            t = lax.dot_general(
                gb[pl.ds(at, grp_rows), :], weights, (((1,), (1,)), ((), ())),
                preferred_element_type=jnp.float32,
            )
            t = jnp.where(own, t, 0.0).astype(jnp.bfloat16)
            s = jnp.dot(t, weights, preferred_element_type=jnp.float32)
            for pair in range(pairs):
                piece = s[:, pair * LANES:(pair + 1) * LANES]
                z2[pair, pl.ds(at, grp_rows), :] = piece
                z2[pair, pl.ds(all_rows + at, grp_rows), :] = piece
            return carry

        lax.fori_loop(0, local_blocks // group, one, 0, unroll=4)
        begin = [
            lax.rem(2 * blocks - off[k] - row * local_blocks, blocks) * loads for k in range(2 * pairs)
        ]
        tall = 64
        for c in range(all_rows // tall):
            sums = [0.0, 0.0]
            for pair in range(pairs):
                for e in range(2):
                    sums[e] = sums[e] + z2[pair, pl.ds(begin[2 * pair + e] + c * tall, tall), :]
            both = jnp.where(low, sums[0], sums[1])
            un[c * tall:(c + 1) * tall, :] = both + pltpu.roll(both, block, 1)
        for l in range(loads):
            even = un[pl.ds(l, whole, stride=wide), :]
            odd = un[pl.ds(loads + l, whole, stride=wide), :]
            out[l] = jnp.where(low, even, odd).reshape(rows, half, LANES)
        for l in range(loads):
            out[l, row] = out[l, row] + sd[...] * x[l, row]

    def precondition(x, phase, out):
        mine = part.at[phase]
        schur(x, mine)
        copies = [
            sibling(mine, sib.at[phase, d - 1], d, ps_s.at[phase, d], ps_r.at[phase, d])
            for d in range(1, rows)
        ]
        for copy in copies:
            copy.start()
        for copy in copies:
            copy.wait()
        total = ss.at[phase]
        for l in range(loads):
            value = mine[l]
            for d in range(rows - 1):
                value = value + sib[phase, d, l]
            total[l] = value

        def halo(f, to):
            return across(
                total.at[:, :, span(f)], ac.at[phase, :, :, span(to)], f, 0,
                hs_s.at[phase, f], hs_r.at[phase, to],
            )

        for f in range(4):

            @pl.when(opened[f])
            def _():
                halo(f, OPPOSITE[f]).start()

        for f in range(4):

            @pl.when(opened[f])
            def _():
                halo(f, f).wait()

        jump(total, ac.at[phase], out)

    lane = lax.broadcasted_iota(jnp.int32, (loads, padded), 1)

    def total_of(values):
        flat = jnp.concatenate(
            [jnp.sum(values[l].reshape(whole, LANES), axis=0, keepdims=True) for l in range(loads)], axis=0
        )
        return jnp.sum(flat, axis=1, keepdims=True)

    def assemble(phase, direction):
        z = zz[...]
        out = jnp.zeros((loads, padded), jnp.float32)
        for q in range(slots):
            out = out + total_of(z * fbf[1 + q][None]) * tf[q:q + 1, :]
        flexed = z * fbf[0][None]
        energies = [total_of(rs[...] * z), total_of(flexed * z)]
        if direction is not None:
            energies.append(total_of(flexed * direction[...]))
        for e, value in enumerate(energies):
            out = out + jnp.where(lane == coarse + e, value, 0.0)
        msg[phase] = out
        ar[phase, me] = out

        def send(d, slot):
            return pltpu.make_async_remote_copy(
                src_ref=msg.at[phase], dst_ref=ar.at[phase, slot],
                send_sem=as_s.at[phase, d], recv_sem=as_r.at[phase, d],
                device_id={"sub": (me + d) % subs, "row": row}, device_id_type=MESH,
            )

        def start(d, carry):
            send(d, me).start()
            return carry

        def wait(d, carry):
            send(d, (me - d + subs) % subs).wait()
            return carry

        lax.fori_loop(1, subs, start, 0)
        lax.fori_loop(1, subs, wait, 0)
        total = jnp.sum(ar[phase], axis=0)
        picked = [
            jnp.sum(jnp.where(lane == coarse + e, total, 0.0), axis=1, keepdims=True)
            for e in range(len(energies))
        ]
        return jnp.where(lane < coarse, total, 0.0), picked

    def spread_of(coarse_half, l):
        return jnp.sum(tf[...] * coarse_half[l:l + 1, :], axis=1, keepdims=True)

    def update(coarse_half, step, run_rows, direction, apply):
        for l in range(loads):
            back = spread_of(coarse_half, l)
            mine = [jnp.broadcast_to(back[q:q + 1, :], (face, LANES)) for q in range(slots)]
            scale = jnp.broadcast_to(step[l:l + 1, :], (face, LANES))
            for f in range(4):
                at = slice(f * face, (f + 1) * face)
                base = (1 + f) * SLOT
                theirs = [
                    jnp.broadcast_to(back[base + q:base + q + 1, :], (face, LANES)) for q in range(slots)
                ]
                for r in run_rows:
                    p = direction(l, r, at)
                    image = fsum[r, at, :] * p
                    for q in range(slots):
                        image = image + (mine[q] * fbf[1 + q, r, at, :] - theirs[q] * fba[1 + q, r, at, :])
                    apply(l, r, at, scale, p, jnp.where(faces[f], image, 0.0))

    own_gap.wait()
    exchange_wait(*first)
    jump(gapf, ac_gap, rs)
    load_off.wait()
    load_sd.wait()
    load_factor.wait()
    precondition(rs, 0, zz)
    exchange_wait(*second)
    fsum[...] = fbf[0] + fba[0]
    coarse_half, (res_dot, energy) = assemble(0, None)

    def curvature(energy, coarse_half):
        return 2.0 * (energy + jnp.sum(coarse_half * coarse_half, axis=1, keepdims=True))

    step = res_dot / curvature(energy, coarse_half)
    pp[...] = zz[...]

    def apply_first(l, r, at, scale, p, image):
        mm[l, r, at, :] = scale * p
        rs[l, r, at, :] = rs[l, r, at, :] - scale * image

    update(coarse_half, step, range(rows), lambda l, r, at: pp[l, r, at, :], apply_first)
    precondition(rs, 1, zz)
    new_half, (res_new, energy_new, mixed) = assemble(1, pp)
    ratio = res_new / res_dot
    energy = energy_new + 2.0 * ratio * mixed + ratio * ratio * energy
    coarse_half = new_half + ratio * coarse_half
    step = res_new / curvature(energy, coarse_half)

    def last_direction(l, r, at):
        return zz[l, r, at, :] + ratio[l:l + 1, :] * pp[l, r, at, :]

    def apply_last(l, r, at, scale, p, image):
        mult_out[l, at, :] = mm[l, r, at, :] + scale * p
        res_out[l, at, :] = rs[l, r, at, :] - scale * image

    update(coarse_half, step, (row,), last_direction, apply_last)


def shards(subs, rows, gap_field, flex_diag, schur_diag, schur_factor, block_offsets, coarse_basis, coarse_factor):
    loads, _, unknowns = gap_field.shape
    _, local_blocks, block, width = schur_factor.shape
    slots = coarse_basis.shape[1]
    coarse = coarse_factor.shape[0]
    half = unknowns // LANES
    padded = -(-(coarse + 3) // LANES) * LANES
    gap = gap_field.reshape(loads, half, LANES)
    flex = flex_diag.reshape(half, LANES)
    basis_rows = coarse_basis.reshape(slots, half, LANES)
    sd = schur_diag.reshape(half, LANES)
    factor = schur_factor.reshape(local_blocks * block, width)
    field = (loads, rows, half, LANES)
    basis = (slots + 1, rows, half, LANES)
    all_rows = local_blocks * rows * loads
    f32 = jnp.float32
    vm = pltpu.VMEM
    dma = pltpu.SemaphoreType.DMA
    in_vmem = pl.BlockSpec(memory_space=pltpu.VMEM)
    in_hbm = pl.BlockSpec(memory_space=pltpu.HBM)
    scratch = [
        vm((half, LANES), f32), pltpu.SMEM(block_offsets.shape, jnp.int32), vm(coarse_factor.shape, f32),
        vm(field, f32), vm(field, f32), vm(basis, f32), vm(basis, f32),
        vm(factor.shape, jnp.bfloat16),
        vm((2 * all_rows, LANES), f32),
        vm((local_blocks * loads, width), jnp.bfloat16),
        vm((width // LANES, 2 * all_rows, LANES), f32),
        vm((all_rows, LANES), f32),
        vm(field, f32), vm(field, f32), vm(field, f32), vm(field, f32),
        vm(field[1:], f32),
        vm((2,) + field, f32), vm((2, rows - 1) + field, f32), vm((2,) + field, f32), vm((2,) + field, f32),
        vm((2, loads, padded), f32), vm((2, subs, loads, padded), f32),
        vm((5 * SLOT, padded), f32),
        dma, dma((6,)),
        dma((rows,)), dma((rows,)), dma((4, rows)), dma((4, rows)),
        dma((rows,)), dma((rows,)), dma((4, rows)), dma((4, rows)),
        dma((2, rows)), dma((2, rows)), dma((2, 4)), dma((2, 4)),
        dma((2, subs)), dma((2, subs)),
    ]
    out = jax.ShapeDtypeStruct((loads, half, LANES), f32)
    mult, res = pl.pallas_call(
        functools.partial(kernel, subs, rows, block),
        out_shape=(out, out),
        in_specs=[in_hbm] * 7,
        out_specs=(in_vmem, in_vmem),
        scratch_shapes=scratch,
        compiler_params=pltpu.CompilerParams(
            collective_id=0, has_side_effects=True, vmem_limit_bytes=67_043_328
        ),
    )(gap, flex, basis_rows, sd, factor, block_offsets, coarse_factor)
    return mult.reshape(gap_field.shape), res.reshape(gap_field.shape)


def solution(mesh):
    placed = (
        P(None, "sub", "row"),
        P("sub", "row"),
        P("sub", "row"),
        P("sub", "row", None, None),
        P(),
        P("sub", None, "row"),
        P(),
    )
    return jax.shard_map(
        functools.partial(shards, mesh.shape["sub"], mesh.shape["row"]),
        mesh=mesh,
        in_specs=placed,
        out_specs=(P(None, "sub", "row"), P(None, "sub", "row")),
        check_vma=False,
    )
```

```python
import functools
import jax
import jax.numpy as jnp
from jax import lax
from jax.experimental import pallas as pl
from jax.experimental.pallas import tpu as pltpu
from jax.sharding import PartitionSpec as P

CD = 3
COLS = 4
ITERS = 2
LANES = 128
SLOT = 16
MESH = pl.DeviceIdType.MESH
OPPOSITE = (1, 0, 3, 2)
STEPS = (-1, 1, -COLS, COLS)


def kernel(
    subs, rows, block,
    gap, flex_hbm, basis_hbm, sd_hbm, fac_hbm, off_hbm, cf_hbm,
    mult_out, res_out,
    sd, off, cf, gapf, ac_gap, fbf, fba, fac, xd, gb, z2, un, rs, zz, pp, mm, fsum,
    part, sib, ss, ac, msg, ar, tf,
    fac_sem, own_sem, gs_s, gs_r, gf_s, gf_r, fs_s, fs_r, ff_s, ff_r, fw_s, fw_r,
    ps_s, ps_r, hs_s, hs_r, as_s, as_r,
):
    loads, half = gap.shape[0], gap.shape[1]
    face = half // 4
    slots = basis_hbm.shape[0]
    wide = 2 * loads
    local_rows = gb.shape[0]
    all_rows = local_rows * rows
    blocks = all_rows // loads
    local_blocks = local_rows // loads
    pairs = z2.shape[0]
    whole = half * rows
    coarse = cf.shape[0]
    padded = tf.shape[1]
    me = lax.axis_index("sub")
    row = lax.axis_index("row")
    column = me % COLS
    grid_row = me // COLS
    opened = (column > 0, column < COLS - 1, grid_row > 0, grid_row < subs // COLS - 1)

    load_factor = pltpu.make_async_copy(fac_hbm, fac, fac_sem)
    own_gap = pltpu.make_async_copy(gap, gapf.at[:, row], own_sem.at[0])
    own_flex = pltpu.make_async_copy(flex_hbm, fbf.at[0, row], own_sem.at[1])
    own_basis = pltpu.make_async_copy(basis_hbm, fbf.at[1:, row], own_sem.at[2])
    load_sd = pltpu.make_async_copy(sd_hbm, sd, own_sem.at[3])
    load_off = pltpu.make_async_copy(off_hbm, off, own_sem.at[4])
    load_cf = pltpu.make_async_copy(cf_hbm, cf, own_sem.at[5])
    for copy in (own_gap, own_flex, own_basis, load_off, load_cf, load_sd, load_factor):
        copy.start()

    barrier = pltpu.get_barrier_semaphore()

    def greet(d, carry):
        pl.semaphore_signal(
            barrier, inc=1, device_id={"sub": (me + d) % subs, "row": row}, device_id_type=MESH
        )
        return carry

    lax.fori_loop(1, subs, greet, 0)
    expected = subs - 1 + rows - 1
    for d in range(1, rows):
        other = (row + d) % rows
        pl.semaphore_signal(barrier, inc=1, device_id={"sub": me, "row": other}, device_id_type=MESH)
        for f in range(4):

            @pl.when(opened[f])
            def _():
                pl.semaphore_signal(
                    barrier, inc=1, device_id={"sub": me + STEPS[f], "row": other}, device_id_type=MESH
                )

            expected = expected + jnp.where(opened[f], 1, 0)
    pl.semaphore_wait(barrier, expected)

    def sibling(src, dst, d, sends, receives):
        return pltpu.make_async_remote_copy(
            src_ref=src, dst_ref=dst, send_sem=sends, recv_sem=receives,
            device_id={"sub": me, "row": (row + d) % rows}, device_id_type=MESH,
        )

    def across(src, dst, f, d, sends, receives):
        return pltpu.make_async_remote_copy(
            src_ref=src, dst_ref=dst, send_sem=sends, recv_sem=receives,
            device_id={"sub": me + STEPS[f], "row": (row + d) % rows}, device_id_type=MESH,
        )

    def span(f):
        return pl.ds(f * face, face)

    def exchange_start(src, full, far, sib_s, sib_r, far_s, far_r):
        for d in range(1, rows):
            sibling(src, full.at[:, row], d, sib_s.at[d], sib_r.at[d]).start()
        for f in range(4):

            @pl.when(opened[f])
            def _():
                for d in range(rows):
                    across(
                        src.at[:, span(f)], far.at[:, row, span(OPPOSITE[f])], f, d,
                        far_s.at[f, d], far_r.at[OPPOSITE[f], d],
                    ).start()

    def exchange_wait(src, full, far, sib_s, sib_r, far_s, far_r):
        for d in range(1, rows):
            sibling(src, full.at[:, (row - d + rows) % rows], d, sib_s.at[d], sib_r.at[d]).wait()
        for f in range(4):

            @pl.when(opened[f])
            def _():
                for d in range(rows):
                    across(
                        src.at[:, span(f)], far.at[:, (row - d + rows) % rows, span(f)], f, d,
                        far_s.at[f, d], far_r.at[f, d],
                    ).wait()

    first = (gap, gapf, ac_gap, gs_s, gs_r, gf_s, gf_r)
    exchange_start(*first)

    def basis_sibling(d, sender):
        return sibling(fbf.at[:, row], fbf.at[:, sender], d, fs_s.at[d], fs_r.at[d])

    def basis_across(f, to):
        return across(
            fbf.at[:, row, span(f)], fba.at[:, row, span(to)], f, 0, ff_s.at[f], ff_r.at[to]
        )

    def basis_forward(f, d, sender):
        return sibling(
            fba.at[:, row, span(f)], fba.at[:, sender, span(f)], d, fw_s.at[f, d], fw_r.at[f, d]
        )

    load_cf.wait()

    tf[...] = jnp.zeros_like(tf)
    for n, step in enumerate((0,) + STEPS):
        base_col = (me + step + subs) % COLS if n in (1, 2) else column
        base_row = grid_row + (0 if n < 3 else STEPS[n - 1] // COLS)
        base_row = jnp.clip(base_row, 0, subs // COLS - 1)
        for j in range(4):
            node = (base_row + j // 2) * (COLS + 1) + base_col + j % 2
            for e in range(CD):
                slot = n * SLOT + j * CD + e
                tf[slot:slot + 1, 0:coarse] = cf[pl.ds(node * CD + e, 1), :]
    blank = jnp.zeros((all_rows - local_rows, LANES), jnp.float32)
    for pair in range(pairs):
        z2[pair, local_rows:all_rows, :] = blank
        z2[pair, all_rows + local_rows:2 * all_rows, :] = blank

    for f in range(4):

        @pl.when(jnp.logical_not(opened[f]))
        def _():
            fba[:, :, f * face:(f + 1) * face, :] = jnp.zeros((slots + 1, rows, face, LANES), jnp.float32)

    low = lax.broadcasted_iota(jnp.int32, (1, LANES), 1) < block
    faces = [jnp.full((face, LANES), jnp.where(opened[f], 1, 0), jnp.int32) > 0 for f in range(4)]
    group = 256 // block
    grp_rows = group * loads

    def jump(field, far, out):
        for l in range(loads):
            for r in range(rows):
                for f in range(4):
                    part_f = field[l, r, f * face:(f + 1) * face, :] - far[l, r, f * face:(f + 1) * face, :]
                    out[l, r, f * face:(f + 1) * face, :] = jnp.where(faces[f], part_f, 0.0)

    def schur(x, out, ready):
        for l in range(loads):
            w = x[l].reshape(whole, LANES).astype(jnp.bfloat16).astype(jnp.float32)
            turned = pltpu.roll(w, block, 1)
            even = jnp.where(low, w, turned)
            odd = jnp.where(low, turned, w)
            for copy in range(2):
                xd[pl.ds(copy * all_rows + l, whole, stride=wide), :] = even
                xd[pl.ds(copy * all_rows + loads + l, whole, stride=wide), :] = odd
        for pair in range(pairs):
            at = [(off[2 * pair + e] + row * local_blocks) * loads for e in range(2)]
            left = xd[pl.ds(at[0], local_rows), :]
            right = xd[pl.ds(at[1], local_rows), :]
            gb[:, pair * LANES:(pair + 1) * LANES] = jnp.where(low, left, right).astype(jnp.bfloat16)
        own = (
            lax.broadcasted_iota(jnp.int32, (grp_rows, group * block), 0) // loads
            == lax.broadcasted_iota(jnp.int32, (grp_rows, group * block), 1) // block
        )

        def one(g, carry):
            at = pl.multiple_of(g * grp_rows, grp_rows)
            weights = fac[pl.ds(pl.multiple_of(g * group * block, group * block), group * block), :]
            t = lax.dot_general(
                gb[pl.ds(at, grp_rows), :], weights, (((1,), (1,)), ((), ())),
                preferred_element_type=jnp.float32,
            )
            t = jnp.where(own, t, 0.0).astype(jnp.bfloat16)
            s = jnp.dot(t, weights, preferred_element_type=jnp.float32)
            for pair in range(pairs):
                piece = s[:, pair * LANES:(pair + 1) * LANES]
                z2[pair, pl.ds(at, grp_rows), :] = piece
                z2[pair, pl.ds(all_rows + at, grp_rows), :] = piece
            return carry

        lax.fori_loop(0, local_blocks // group, one, 0, unroll=4)
        begin = [
            lax.rem(2 * blocks - off[k] - row * local_blocks, blocks) * loads for k in range(2 * pairs)
        ]
        tall = face * wide
        for r, f in runs:
            at = (r * 4 + f) * tall
            here = slice(f * face, (f + 1) * face)
            sums = [0.0, 0.0]
            for pair in range(pairs):
                for e in range(2):
                    sums[e] = sums[e] + z2[pair, pl.ds(begin[2 * pair + e] + at, tall), :]
            both = jnp.where(low, sums[0], sums[1])
            un[at:at + tall, :] = both + pltpu.roll(both, block, 1)
            diagonal = jnp.where(row == r, 1.0, 0.0) * sd[here, :]
            for l in range(loads):
                even = un[pl.ds(at + l, face, stride=wide), :]
                odd = un[pl.ds(at + loads + l, face, stride=wide), :]
                out[l, r, here, :] = jnp.where(low, even, odd) + diagonal * x[l, r, here, :]
            ready(r, f)

    runs = [(r, f) for f in range(4) for r in range(rows)]

    def halo(phase, r, f, to):
        return across(
            ss.at[phase, :, r, span(f)], ac.at[phase, :, r, span(to)], f, 0,
            hs_s.at[phase, r, f], hs_r.at[phase, r, to],
        )

    def precondition(x, phase):
        mine = part.at[phase]
        total = ss.at[phase]

        def partial(r, f, d):
            return sibling(
                part.at[phase, :, r, span(f)], sib.at[phase, d - 1, :, r, span(f)], d,
                ps_s.at[phase, d, r, f], ps_r.at[phase, d, r, f],
            )

        def ready(r, f):
            for d in range(1, rows):
                partial(r, f, d).start()

        schur(x, mine, ready)
        for r, f in runs:
            for d in range(1, rows):
                partial(r, f, d).wait()
            here = slice(f * face, (f + 1) * face)
            for l in range(loads):
                value = mine[l, r, here, :]
                for d in range(rows - 1):
                    value = value + sib[phase, d, l, r, here, :]
                total[l, r, here, :] = value

            @pl.when(opened[f])
            def _():
                halo(phase, r, f, OPPOSITE[f]).start()

    def halo_wait(phase, out):
        for r, f in runs:

            @pl.when(opened[f])
            def _():
                halo(phase, r, f, f).wait()

        jump(ss.at[phase], ac.at[phase], out)

    lane = lax.broadcasted_iota(jnp.int32, (loads, padded), 1)

    def total_of(values):
        flat = jnp.concatenate(
            [jnp.sum(values[l].reshape(whole, LANES), axis=0, keepdims=True) for l in range(loads)], axis=0
        )
        return jnp.sum(flat, axis=1, keepdims=True)

    def column_of(values):
        return jnp.sum(jnp.concatenate(values, axis=0), axis=1, keepdims=True)

    def assemble(phase, direction, out_z):
        out = jnp.zeros((loads, padded), jnp.float32)
        flat = [jnp.zeros((1, LANES), jnp.float32) for _ in range(2 * loads)]
        own = [[jnp.zeros((face, LANES), jnp.float32) for _ in range(slots)] for _ in range(loads)]
        for f in range(4):
            here = slice(f * face, (f + 1) * face)
            field = [
                [jnp.where(faces[f], ss[phase, l, r, here, :], 0.0) for r in range(rows)]
                for l in range(loads)
            ]
            for q in range(slots):
                theirs = []
                for l in range(loads):
                    away = 0.0
                    for r in range(rows):
                        own[l][q] = own[l][q] + field[l][r] * fbf[1 + q, r, here, :]
                        away = away + field[l][r] * fba[1 + q, r, here, :]
                    theirs.append(jnp.sum(away, axis=0, keepdims=True))
                slot = (1 + f) * SLOT + q
                out = out - column_of(theirs) * tf[slot:slot + 1, :]
            for l in range(loads):
                dots, mixes = 0.0, 0.0
                for r in range(rows):
                    dots = dots + field[l][r] * rs[l, r, here, :]
                    if direction is not None:
                        mixes = mixes + field[l][r] * fsum[r, here, :] * direction[l, r, here, :]
                flat[l] = flat[l] + jnp.sum(dots, axis=0, keepdims=True)
                if direction is not None:
                    flat[loads + l] = flat[loads + l] + jnp.sum(mixes, axis=0, keepdims=True)
        for q in range(slots):
            sums = [jnp.sum(own[l][q], axis=0, keepdims=True) for l in range(loads)]
            out = out + column_of(sums) * tf[q:q + 1, :]
        out = out + jnp.where(lane == coarse, 2.0 * column_of(flat[:loads]), 0.0)
        energies = 2
        if direction is not None:
            energies = 3
            out = out + jnp.where(lane == coarse + 2, column_of(flat[loads:]), 0.0)
        halo_wait(phase, out_z)
        z = out_z[...]
        out = out + jnp.where(lane == coarse + 1, total_of(z * z * fbf[0][None]), 0.0)
        msg[phase] = out
        ar[phase, me] = out

        def send(d, slot):
            return pltpu.make_async_remote_copy(
                src_ref=msg.at[phase], dst_ref=ar.at[phase, slot],
                send_sem=as_s.at[phase, d], recv_sem=as_r.at[phase, d],
                device_id={"sub": (me + d) % subs, "row": row}, device_id_type=MESH,
            )

        def start(d, carry):
            send(d, me).start()
            return carry

        def wait(d, carry):
            send(d, (me - d + subs) % subs).wait()
            return carry

        lax.fori_loop(1, subs, start, 0)
        lax.fori_loop(1, subs, wait, 0)
        total = jnp.sum(ar[phase], axis=0)
        picked = [
            jnp.sum(jnp.where(lane == coarse + e, total, 0.0), axis=1, keepdims=True)
            for e in range(energies)
        ]
        return jnp.where(lane < coarse, total, 0.0), picked

    def spread_of(coarse_half, l):
        return jnp.sum(tf[...] * coarse_half[l:l + 1, :], axis=1, keepdims=True)

    def update(coarse_half, step, run_rows, direction, apply):
        for l in range(loads):
            back = spread_of(coarse_half, l)
            mine = [jnp.broadcast_to(back[q:q + 1, :], (face, LANES)) for q in range(slots)]
            scale = jnp.broadcast_to(step[l:l + 1, :], (face, LANES))
            for f in range(4):
                at = slice(f * face, (f + 1) * face)
                base = (1 + f) * SLOT
                theirs = [
                    jnp.broadcast_to(back[base + q:base + q + 1, :], (face, LANES)) for q in range(slots)
                ]
                for r in run_rows:
                    p = direction(l, r, at)
                    image = fsum[r, at, :] * p
                    for q in range(slots):
                        image = image + (mine[q] * fbf[1 + q, r, at, :] - theirs[q] * fba[1 + q, r, at, :])
                    apply(l, r, at, scale, p, jnp.where(faces[f], image, 0.0))

    own_gap.wait()
    exchange_wait(*first)
    own_flex.wait()
    own_basis.wait()
    for d in range(1, rows):
        basis_sibling(d, row).start()
    for f in range(4):

        @pl.when(opened[f])
        def _():
            basis_across(f, OPPOSITE[f]).start()

    jump(gapf, ac_gap, rs)
    load_off.wait()
    load_sd.wait()
    load_factor.wait()
    precondition(rs, 0)
    for f in range(4):

        @pl.when(opened[f])
        def _():
            basis_across(f, f).wait()
            for d in range(1, rows):
                basis_forward(f, d, row).start()

    for d in range(1, rows):
        basis_sibling(d, (row - d + rows) % rows).wait()
    for f in range(4):

        @pl.when(opened[f])
        def _():
            for d in range(1, rows):
                basis_forward(f, d, (row - d + rows) % rows).wait()

    fsum[...] = fbf[0] + fba[0]
    coarse_half, (res_dot, energy) = assemble(0, None, pp)

    def curvature(energy, coarse_half):
        return 2.0 * (energy + jnp.sum(coarse_half * coarse_half, axis=1, keepdims=True))

    step = res_dot / curvature(energy, coarse_half)

    def apply_first(l, r, at, scale, p, image):
        mm[l, r, at, :] = scale * p
        rs[l, r, at, :] = rs[l, r, at, :] - scale * image

    update(coarse_half, step, range(rows), lambda l, r, at: pp[l, r, at, :], apply_first)
    precondition(rs, 1)
    new_half, (res_new, energy_new, mixed) = assemble(1, pp, zz)
    ratio = res_new / res_dot
    energy = energy_new + 2.0 * ratio * mixed + ratio * ratio * energy
    coarse_half = new_half + ratio * coarse_half
    step = res_new / curvature(energy, coarse_half)

    def last_direction(l, r, at):
        return zz[l, r, at, :] + ratio[l:l + 1, :] * pp[l, r, at, :]

    def apply_last(l, r, at, scale, p, image):
        mult_out[l, at, :] = mm[l, r, at, :] + scale * p
        res_out[l, at, :] = rs[l, r, at, :] - scale * image

    update(coarse_half, step, (row,), last_direction, apply_last)


def shards(subs, rows, gap_field, flex_diag, schur_diag, schur_factor, block_offsets, coarse_basis, coarse_factor):
    loads, _, unknowns = gap_field.shape
    _, local_blocks, block, width = schur_factor.shape
    slots = coarse_basis.shape[1]
    coarse = coarse_factor.shape[0]
    half = unknowns // LANES
    padded = -(-(coarse + 3) // LANES) * LANES
    gap = gap_field.reshape(loads, half, LANES)
    flex = flex_diag.reshape(half, LANES)
    basis_rows = coarse_basis.reshape(slots, half, LANES)
    sd = schur_diag.reshape(half, LANES)
    factor = schur_factor.reshape(local_blocks * block, width)
    field = (loads, rows, half, LANES)
    basis = (slots + 1, rows, half, LANES)
    all_rows = local_blocks * rows * loads
    f32 = jnp.float32
    vm = pltpu.VMEM
    dma = pltpu.SemaphoreType.DMA
    in_vmem = pl.BlockSpec(memory_space=pltpu.VMEM)
    in_hbm = pl.BlockSpec(memory_space=pltpu.HBM)
    scratch = [
        vm((half, LANES), f32), pltpu.SMEM(block_offsets.shape, jnp.int32), vm(coarse_factor.shape, f32),
        vm(field, f32), vm(field, f32), vm(basis, f32), vm(basis, f32),
        vm(factor.shape, jnp.bfloat16),
        vm((2 * all_rows, LANES), f32),
        vm((local_blocks * loads, width), jnp.bfloat16),
        vm((width // LANES, 2 * all_rows, LANES), f32),
        vm((all_rows, LANES), f32),
        vm(field, f32), vm(field, f32), vm(field, f32), vm(field, f32),
        vm(field[1:], f32),
        vm((2,) + field, f32), vm((2, rows - 1) + field, f32), vm((2,) + field, f32), vm((2,) + field, f32),
        vm((2, loads, padded), f32), vm((2, subs, loads, padded), f32),
        vm((5 * SLOT, padded), f32),
        dma, dma((6,)),
        dma((rows,)), dma((rows,)), dma((4, rows)), dma((4, rows)),
        dma((rows,)), dma((rows,)), dma((4,)), dma((4,)), dma((4, rows)), dma((4, rows)),
        dma((2, rows, rows, 4)), dma((2, rows, rows, 4)), dma((2, rows, 4)), dma((2, rows, 4)),
        dma((2, subs)), dma((2, subs)),
    ]
    out = jax.ShapeDtypeStruct((loads, half, LANES), f32)
    mult, res = pl.pallas_call(
        functools.partial(kernel, subs, rows, block),
        out_shape=(out, out),
        in_specs=[in_hbm] * 7,
        out_specs=(in_vmem, in_vmem),
        scratch_shapes=scratch,
        compiler_params=pltpu.CompilerParams(
            collective_id=0, has_side_effects=True, vmem_limit_bytes=67_043_328
        ),
    )(gap, flex, basis_rows, sd, factor, block_offsets, coarse_factor)
    return mult.reshape(gap_field.shape), res.reshape(gap_field.shape)


def solution(mesh):
    placed = (
        P(None, "sub", "row"),
        P("sub", "row"),
        P("sub", "row"),
        P("sub", "row", None, None),
        P(),
        P("sub", None, "row"),
        P(),
    )
    return jax.shard_map(
        functools.partial(shards, mesh.shape["sub"], mesh.shape["row"]),
        mesh=mesh,
        in_specs=placed,
        out_specs=(P(None, "sub", "row"), P(None, "sub", "row")),
        check_vma=False,
    )
```
